256 devices in a mesh: wide: 32 (over z, x_hi, core), dp: 8 (over y, x_lo).
Axes of the slice: x: 4 (x_hi: 2, x_lo: 2; x = x_hi * 2 + x_lo), y: 4, z: 8, core: 2. Of those that a mesh axis runs over, the one named last changes fastest.
Arguments:
- queries: bfloat16 [131072, 4096], P(('wide', 'dp')), may hold values from -20 to 20
- teacher_queries: bfloat16 [131072, 4096], P(('wide', 'dp')), may hold values from -6 to 6
- passages: bfloat16 [512, 4096], P('wide'), may hold values from -6 to 6
- bank_student: bfloat16 [8192, 4096], P('wide'), may hold values from -6 to 6
- bank_teacher: bfloat16 [8192, 4096], P('wide'), may hold values from -6 to 6
- owner: int32 [8], P('dp'), may hold values from 0 to 31
- positives: int32 [131072], P(('wide', 'dp')), may hold values from 0 to 511
- keep_mask: int32 [131072, 256], P(('wide', 'dp')), may hold values 0 or 1
Outputs:
- row_loss: float32 [131072], P(('wide', 'dp'))
- query_grad: bfloat16 [131072, 4096], P(('wide', 'dp'))
- passage_grad: float32 [512, 4096], P('wide')
The draws below stay inside these ranges and needn't reach their ends.
All inputs are finite; a program needn't handle non-finite values. No bound on the sum of `keep_mask` on one device may be relied on, other than what follows from the above.
Results may differ from the reference program's by a relative error of at most 0.0033.
Values may be sent and summed in bfloat16 or wider, within the bound.
A program may use at most 128 MiB of HBM per device.

```python
import math
import jax
import jax.numpy as jnp
from jax import lax

E = 4096
QDEV = 512
POOL = 256
NP = 512
QN = 131072
BANK = 8192
N_WIDE = 32
N_DP = 8


def draw_pair(key):
    base = jax.random.fold_in(key, 11)
    key_a, key_b = jax.random.split(base, 2)
    passages = jnp.clip(jax.random.normal(key_a, (NP, E), jnp.float32), -4.0, 4.0)
    queries = jnp.clip(jax.random.normal(key_b, (QN, E), jnp.float32), -4.0, 4.0)
    return (queries, passages)


def draw_queries(key, part):
    return draw_pair(key)[0].astype(jnp.bfloat16)


def draw_passages(key, part):
    return draw_pair(key)[1].astype(jnp.bfloat16)


def place_ends(drawn, stream_key, smallest, high):
    longest = drawn.shape.index(max(drawn.shape))
    spots = []
    for shift in (0, 1):
        where = [jax.random.randint(jax.random.fold_in(stream_key, axis), (), 0, length) for axis, length in enumerate(drawn.shape)]
        where[longest] = (where[longest] + shift) % drawn.shape[longest]
        spots.append(tuple(where))
    return drawn.at[spots[0]].set(smallest).at[spots[1]].set(high)


def block_levels(rng, extent, shards, least, top_value):
    factor_of, own = 1.0, jax.random.fold_in(rng, 6)
    for dim, parts in shards:
        steps = jnp.exp(jax.random.uniform(jax.random.fold_in(own, dim), (parts,), jnp.float32, least / len(shards), top_value / len(shards)))
        factor_of = factor_of * jnp.repeat(steps, extent[dim] // parts).reshape([-1 if axis == dim else 1 for axis in range(len(extent))])
    return factor_of


def gaussian(own_key, extent, scale, reach, cuts=(), held_as=jnp.bfloat16):
    entries = scale * jax.random.normal(own_key, extent, jnp.float32)
    if cuts:
        entries = entries * block_levels(own_key, extent, cuts, -0.22, 0.18)
    return jnp.clip(entries, -reach, reach).astype(held_as)


def setup_inputs(seed: int = 0) -> dict:
    key_list = jax.random.split(jax.random.key(seed), 9)
    queries = draw_queries(jax.random.fold_in(key_list[8], 71), 0)
    teacher_queries = gaussian(key_list[1], (QN, E), 1.0, 6.0, ((0, 256),))
    passages = draw_passages(jax.random.fold_in(key_list[8], 71), 0)
    bank_student = gaussian(key_list[3], (BANK, E), 1.0, 6.0, ((0, 32),))
    bank_teacher = gaussian(key_list[4], (BANK, E), 1.0, 6.0, ((0, 32),))
    owner = place_ends(jax.random.randint(key_list[5], (N_DP,), 0, N_WIDE), jax.random.fold_in(key_list[5], 1), 0, N_WIDE - 1).astype(jnp.int32)
    positives = place_ends(jax.random.randint(key_list[6], (QN,), 0, NP), jax.random.fold_in(key_list[6], 1), 0, NP - 1).astype(jnp.int32)
    keep_mask = place_ends((jax.random.randint(key_list[7], (QN, POOL), 0, 2) < 1).astype(jnp.int32), jax.random.fold_in(key_list[7], 1), 0, 1)
    return {"queries": queries, "teacher_queries": teacher_queries, "passages": passages, "bank_student": bank_student, "bank_teacher": bank_teacher, "owner": owner, "positives": positives, "keep_mask": keep_mask}


def reference(queries, teacher_queries, passages, bank_student, bank_teacher, owner, positives, keep_mask):
    scale = 2.0 / math.sqrt(E)
    count = QN // QDEV
    query_blocks = queries.reshape(count, QDEV, E)
    teacher_blocks = teacher_queries.reshape(count, QDEV, E)
    pos_blocks = positives.reshape(count, QDEV)
    mask_blocks = keep_mask.reshape(count, QDEV, POOL)
    block_ids = jnp.arange(count, dtype=jnp.int32)
    columns = jnp.arange(NP, dtype=jnp.int32)

    def one_block(carry, items):
        query, teacher, pos, keep, block_id = items
        replica = (block_id % N_DP).astype(jnp.int32)
        first = (owner[replica].astype(jnp.int32) * POOL).astype(jnp.int32)
        pool_s = lax.dynamic_slice_in_dim(bank_student, first, POOL, 0)
        pool_t = lax.dynamic_slice_in_dim(bank_teacher, first, POOL, 0)
        zp = jnp.dot(query, passages.T, preferred_element_type=jnp.float32) * scale
        zq = jnp.dot(query, pool_s.T, preferred_element_type=jnp.float32) * scale
        tt = jnp.dot(teacher, pool_t.T, preferred_element_type=jnp.float32) * scale
        weight = keep.astype(jnp.float32) * jax.nn.sigmoid(-tt)
        top = jnp.maximum(lax.optimization_barrier(jnp.max(zp, axis=1)), lax.optimization_barrier(jnp.max(zq, axis=1)))
        total = lax.optimization_barrier(jnp.sum(jnp.exp(zp - top[:, None]), axis=1)) + lax.optimization_barrier(jnp.sum(weight * jnp.exp(zq - top[:, None]), axis=1))
        lse = top + jnp.log(total)
        hit = (columns[None, :] == pos[:, None]).astype(jnp.float32)
        loss = lse - lax.optimization_barrier(jnp.sum(zp * hit, axis=1))
        grad_p = (jnp.exp(zp - lse[:, None]) - hit).astype(jnp.bfloat16)
        grad_q = (weight * jnp.exp(zq - lse[:, None])).astype(jnp.bfloat16)
        qgrad = (jnp.dot(grad_p, passages, preferred_element_type=jnp.float32) + jnp.dot(grad_q, pool_s, preferred_element_type=jnp.float32)) * scale
        carry = carry + lax.dot_general(grad_p, query, (((0,), (0,)), ((), ())), preferred_element_type=jnp.float32)
        return (carry, (loss, qgrad.astype(jnp.bfloat16)))
    start = jnp.zeros((NP, E), jnp.float32)
    summed, (losses, qgrads) = lax.scan(one_block, start, (query_blocks, teacher_blocks, pos_blocks, mask_blocks, block_ids))
    return (losses.reshape(QN), qgrads.reshape(QN, E), summed * scale)
```

```python
import math

import jax
import jax.numpy as jnp
from jax import lax
from jax.sharding import Mesh
from jax.experimental import pallas as pl
from jax.experimental.pallas import tpu as pltpu
from jax.sharding import PartitionSpec as P

E = 4096
WIDE = ("z", "xh", "c")
DP = ("y", "xl")
AXES = WIDE + DP
WIDE_DP = AXES
MESH = pl.DeviceIdType.MESH


def pool_broadcast(PARTS, L):
    n = PARTS * 16
    cw = 4096 // PARTS
    S = n + 15 * L

    def kernel(own_ref, bs, bt, ps, pt, own, oth, R, C, O, lsem, xs, xr, ss, rs, ds, dr):
        z, xh, c, y, xl = [lax.axis_index(a) for a in AXES]
        off = 4 * xl
        q = lax.rem(z - off + 8, 8)
        p = xh * 7 * 0 + (1 - xh) * q + xh * (15 - q)
        d = 1 - 2 * c
        def coords(pp):
            h = pp // 8
            qq = (1 - h) * pp + h * (15 - pp)
            return lax.rem(qq + off, 8), h
        zn, hn = coords(lax.rem(p + d + 16, 16))
        zp, hp = coords(lax.rem(p - d + 16, 16))
        nxt = {"z": zn, "xh": hn}
        prv = {"z": zp, "xh": hp}
        peer = {"c": 1 - c}
        bar = pltpu.get_barrier_semaphore()
        for dev in (nxt, prv, peer):
            pl.semaphore_signal(bar, inc=1, device_id=dev, device_id_type=MESH)

        def loads(src):
            return [pltpu.make_async_copy(src.at[:, pl.ds(i * cw, cw)], own.at[i], lsem.at[i]) for i in range(PARTS)]
        def xch(src):
            return [pltpu.make_async_remote_copy(src.at[:, pl.ds(i * cw, cw)], oth.at[i], xs.at[i], xr.at[i], device_id=peer, device_id_type=MESH) for i in range(PARTS)]

        @pl.when(c == 0)
        def _():
            for k in loads(bs): k.start()
        @pl.when(c == 1)
        def _():
            for k in loads(bt): k.start()
        pl.semaphore_wait(bar, 3)
        @pl.when(c == 0)
        def _():
            for k in xch(bt): k.start()
        @pl.when(c == 1)
        def _():
            for k in xch(bs): k.start()

        o = own_ref[0]
        oz, oh, oc = o // 4, lax.rem(o // 2, 2), lax.rem(o, 2)
        oq = lax.rem(oz - off + 8, 8)
        op = (1 - oh) * oq + oh * (15 - oq)
        mine = jnp.logical_and(op == p, oc == c)
        other = jnp.logical_and(op == p, oc == 1 - c)
        fv = lax.rem(p - op + 16, 16)
        bv = lax.rem(op - p + 16, 16)
        v = jnp.where(c == 0, fv, bv)
        vo = jnp.where(c == 0, bv, fv)

        def ring(s):
            return pltpu.make_async_remote_copy(C.at[s], R.at[s], ss.at[s], rs.at[s], device_id=nxt, device_id_type=MESH)
        def d2d(s):
            return pltpu.make_async_remote_copy(C.at[s], O.at[s], ds.at[s], dr.at[s], device_id=peer, device_id_type=MESH)
        def inj(s):
            part = s // 16
            rows = pl.ds(pl.multiple_of(lax.rem(s, 16) * 16, 16), 16)
            return own[part, rows, :], oth[part, rows, :]
        def waitx(i):
            pltpu.make_async_copy(own.at[i], own.at[i], lsem.at[i]).wait()
            pltpu.make_async_remote_copy(oth.at[i], oth.at[i], xs.at[i], xr.at[i], device_id=peer, device_id_type=MESH).wait()
        assert L <= 16
        for i in range(PARTS):
            waitx(i)
            def body1(s, _):
                a, b = inj(s)
                C[s] = jnp.where(mine, a, b)
                ring(s).start(); d2d(s).start()
                return 0
            def body2(s, _):
                a, b = inj(s)
                ring(s - L).wait_recv()
                C[s] = jnp.where(mine, a, jnp.where(other, b, R[s - L]))
                ring(s).start(); d2d(s).start()
                return 0
            lo = 16 * i
            if i == 0:
                lax.fori_loop(0, L, body1, 0)
                lo = L
            lax.fori_loop(lo, 16 * i + 16, body2, 0)
        def body3(s, _):
            ring(s - L).wait_recv()
            C[s] = R[s - L]
            ring(s).start(); d2d(s).start()
            return 0
        lax.fori_loop(n, S - L, body3, 0)
        def body4(s, _):
            ring(s - L).wait_recv()
            C[s] = R[s - L]
            d2d(s).start()
            return 0
        lax.fori_loop(S - L, S, body4, 0)
        def fin(s, _):
            ring(s).wait_send()
            return 0
        lax.fori_loop(0, S - L, fin, 0)
        def fin2(s, _):
            d2d(s).wait()
            return 0
        lax.fori_loop(0, S, fin2, 0)
        for i in range(PARTS):
            A = C[pl.ds(v * L + 16 * i, 16)].reshape(256, cw)
            B = O[pl.ds(vo * L + 16 * i, 16)].reshape(256, cw)
            ps[:, pl.ds(i * cw, cw)] = jnp.where(c == 0, A, B)
            pt[:, pl.ds(i * cw, cw)] = jnp.where(c == 0, B, A)

    def call(owner, bs, bt):
        return pl.pallas_call(
            kernel,
            out_shape=[jax.ShapeDtypeStruct((256, 4096), jnp.bfloat16)] * 2,
            in_specs=[pl.BlockSpec(memory_space=pltpu.SMEM), pl.BlockSpec(memory_space=pl.ANY), pl.BlockSpec(memory_space=pl.ANY)],
            out_specs=[pl.BlockSpec(memory_space=pltpu.VMEM)] * 2,
            scratch_shapes=[
                pltpu.VMEM((PARTS, 256, cw), jnp.bfloat16),
                pltpu.VMEM((PARTS, 256, cw), jnp.bfloat16),
                pltpu.VMEM((S - L, 16, cw), jnp.bfloat16),
                pltpu.VMEM((S, 16, cw), jnp.bfloat16),
                pltpu.VMEM((S, 16, cw), jnp.bfloat16),
                pltpu.SemaphoreType.DMA((PARTS,)),
                pltpu.SemaphoreType.DMA((PARTS,)),
                pltpu.SemaphoreType.DMA((PARTS,)),
                pltpu.SemaphoreType.DMA((S - L,)),
                pltpu.SemaphoreType.DMA((S - L,)),
                pltpu.SemaphoreType.DMA((S,)),
                pltpu.SemaphoreType.DMA((S,)),
            ],
            compiler_params=pltpu.CompilerParams(collective_id=0, has_side_effects=True, vmem_limit_bytes=48 << 20),
            name=f"pool_{PARTS}_{L}",
        )(owner, bs, bt)
    return call

def laid_out(tiles, dim):
    tiles = jnp.moveaxis(tiles, 0, dim)
    shape = tiles.shape
    return tiles.reshape(*shape[:dim], shape[dim] * shape[dim + 1], *shape[dim + 2 :])


def all_blocks(value, axes, order):
    tiles = value
    for k in order:
        tiles = lax.all_gather(tiles, axes[k])
    done = order[::-1]
    back = [done.index(k) for k in range(len(axes))]
    tiles = tiles.transpose(*back, *range(len(axes), tiles.ndim))
    return tiles.reshape(-1, *value.shape)


def whole_of(value, axes, order, dim):
    return laid_out(all_blocks(value, axes, order), dim)


def own_block(tiles, axes, order):
    shape = [lax.axis_size(a) for a in axes]
    tiles = tiles.reshape(*shape, *tiles.shape[1:])
    tiles = tiles.transpose(*order, *range(len(axes), tiles.ndim))
    tiles = tiles.reshape(-1, *tiles.shape[len(axes) :])
    for k in order:
        tiles = lax.psum_scatter(tiles, axes[k], scatter_dimension=0, tiled=True)
    return tiles[0]


def split_up(value, dim, devices):
    before, after = (value.shape[:dim], value.shape[dim + 1 :])
    return jnp.moveaxis(value.reshape(*before, devices, -1, *after), dim, 0)


def summed_rows_2(value, axes, order, dim):
    devices = lax.axis_size(axes)
    return own_block(split_up(value, dim, devices), axes, order)


def from_everyone(value, axis):
    copies = jnp.broadcast_to(value, (lax.axis_size(axis), *value.shape))
    return lax.all_to_all(copies, axis, split_axis=0, concat_axis=0, tiled=True)


def over_copies(value, axis):
    return from_everyone(value, axis).sum(axis=0)


def body(
    queries, teacher_queries, passages, bank_student, bank_teacher, owner, positives, keep_mask
):
    scale = 2.0 / math.sqrt(E)
    block = passages.shape[0]
    cycle_size = lax.axis_size(WIDE)
    total_rows = block * cycle_size
    pool_s, pool_t = pool_broadcast(4, 8)(owner, bank_student, bank_teacher)
    zq = jnp.dot(queries, pool_s.T, preferred_element_type=jnp.float32) * scale
    tt = jnp.dot(teacher_queries, pool_t.T, preferred_element_type=jnp.float32) * scale
    weight = keep_mask.astype(jnp.float32) * jax.nn.sigmoid(-tt)
    pool_top = jnp.max(zq, axis=1)
    pool_total = jnp.sum(weight * jnp.exp(zq - pool_top[:, None]), axis=1)
    piece = whole_of(passages, WIDE, (1, 0, 2), 0)
    run_top = pool_top
    run_total = pool_total
    scores = jnp.dot(queries, piece.T, preferred_element_type=jnp.float32) * scale
    new_top = jnp.maximum(run_top, jnp.max(scores, axis=1))
    run_total = run_total * jnp.exp(run_top - new_top) + jnp.sum(
        jnp.exp(scores - new_top[:, None]), axis=1
    )
    score_store = scores
    passage_store = piece
    run_top, run_total, score_store, passage_store = (
        new_top,
        run_total,
        score_store,
        passage_store,
    )
    lse = run_top + jnp.log(run_total)
    columns = jnp.arange(total_rows, dtype=jnp.int32)
    hit = (columns[None, :] == positives[:, None]).astype(jnp.float32)
    row_loss = lse - jnp.sum(score_store * hit, axis=1)
    grad_p = (jnp.exp(score_store - lse[:, None]) - hit).astype(jnp.bfloat16)
    grad_q = (weight * jnp.exp(zq - lse[:, None])).astype(jnp.bfloat16)
    qgrad = jnp.dot(grad_p, passage_store, preferred_element_type=jnp.float32) + jnp.dot(
        grad_q, pool_s, preferred_element_type=jnp.float32
    )
    local_sums = summed_rows_2(
        lax.dot_general(
            grad_p, queries, (((0,), (0,)), ((), ())), preferred_element_type=jnp.float32
        ),
        WIDE,
        (2, 0, 1),
        0,
    )
    passage_grad = over_copies(local_sums, DP) * scale
    query_grad = (qgrad * scale).astype(jnp.bfloat16)
    return (row_loss, query_grad, passage_grad)


def solution(mesh):
    torus = Mesh(
        mesh.devices.reshape(8, 2, 2, 4, 2), AXES
    )
    in_specs = (
        P(WIDE_DP, None),
        P(WIDE_DP, None),
        P(WIDE, None),
        P(WIDE, None),
        P(WIDE, None),
        P(DP),
        P(WIDE_DP),
        P(WIDE_DP, None),
    )
    out_specs = (P(WIDE_DP), P(WIDE_DP, None), P(WIDE, None))
    return jax.shard_map(body, mesh=torus, in_specs=in_specs, out_specs=out_specs, check_vma=False)
```

```python
import math

import jax
import jax.numpy as jnp
from jax import lax
from jax.experimental import pallas as pl
from jax.experimental.pallas import tpu as pltpu
from jax.sharding import Mesh
from jax.sharding import PartitionSpec as P

E = 4096
WIDE = ("z", "xh", "c")
DP = ("y", "xl")
AXES = WIDE + DP
MESH = pl.DeviceIdType.MESH
SCALE = 2.0 / math.sqrt(E)
BF = jnp.bfloat16
F32 = jnp.float32

PARTS = 4
CW = E // PARTS
N = PARTS * 16
L = 8
L2 = 12
S = N + 8 * L + L2
BATCH = 4
NB = S // BATCH
assert S % BATCH == 0
EDGES = sorted({0, L, L2, N, N + L, N + L + L2, S - L, S} | {16 * i for i in range(PARTS)})

NT = (((1,), (1,)), ((), ()))


def dot(a, b):
    return jnp.dot(a, b, preferred_element_type=F32)


def dot_nt(a, b):
    return lax.dot_general(a, b, NT, preferred_element_type=F32)


def kernel(
    owner_ref, q_hbm, t_hbm, p_hbm, bs_hbm, bt_hbm, pos_ref, keep_ref,
    loss_ref, qg_hbm, pg_ref,
    q, t, pa, own, oth, ring_in, rung_in, stream,
    zp_t, zq_t, tt_t, gp_t, gp, gq,
    give, got, kept, merged, first_y, first_x, second_out, second_in, piece, third_in,
    load_sem, own_sem, oth_s, oth_r, ring_s, ring_r, rung_s, rung_r, share_s, share_r,
    pz_s, pz_r, px_s, px_r, py_s, py_r, pc_s, pc_r,
    gc_s, gc_r, g1_s, g1_r, g2_s, g2_r, g3_s, g3_r, g4_s, g4_r, out_sem,
):
    z, xh, c, y, xl = [lax.axis_index(a) for a in AXES]
    x = xh * 2 + xl

    def along_x(j):
        other = lax.rem(x + j, 4)
        return {"xh": other // 2, "xl": lax.rem(other, 2)}

    zs = {j: {"z": lax.rem(z + j, 8)} for j in range(1, 8)}
    xs = {j: along_x(j) for j in range(1, 4)}
    ys = {j: {"y": lax.rem(y + j, 4)} for j in range(1, 4)}
    peer = {"c": 1 - c}
    dps = {
        2 * a + b: {"y": lax.rem(y + a, 4), "xl": lax.rem(xl + b, 2)}
        for a in range(4)
        for b in range(2)
        if a or b
    }

    def send(src, dst, send_sem, recv_sem, device):
        return pltpu.make_async_remote_copy(
            src, dst, send_sem, recv_sem, device_id=device, device_id_type=MESH
        )

    barrier = pltpu.get_barrier_semaphore()
    greeted = [*zs.values(), *xs.values(), peer, *[dps[k] for k in dps if k != 1]]
    for device in greeted:
        pl.semaphore_signal(barrier, inc=1, device_id=device, device_id_type=MESH)

    pcol = pl.multiple_of(y * 1024 + xl * 512, 512)
    prow = pl.multiple_of(xh * 128 + z * 16, 16)
    mine_p = pa.at[c, pl.ds(prow, 16), pl.ds(pcol, 512)]
    load_p = pltpu.make_async_copy(p_hbm.at[:, pl.ds(pcol, 512)], mine_p, load_sem.at[2])
    load_p.start()

    def own_loads(src):
        return [
            pltpu.make_async_copy(src.at[:, pl.ds(i * CW, CW)], own.at[i], own_sem.at[i])
            for i in range(PARTS)
        ]

    def other_loads(src):
        return [
            send(src.at[:, pl.ds(i * CW, CW)], oth.at[i], oth_s.at[i], oth_r.at[i], peer)
            for i in range(PARTS)
        ]

    @pl.when(c == 0)
    def _():
        for k in own_loads(bs_hbm):
            k.start()

    @pl.when(c == 1)
    def _():
        for k in own_loads(bt_hbm):
            k.start()

    load_q = pltpu.make_async_copy(q_hbm, q, load_sem.at[0])
    load_t = pltpu.make_async_copy(t_hbm, t, load_sem.at[1])
    pl.semaphore_wait(barrier, len(greeted))

    @pl.when(c == 0)
    def _():
        for k in other_loads(bt_hbm):
            k.start()

    @pl.when(c == 1)
    def _():
        for k in other_loads(bs_hbm):
            k.start()

    load_p.wait()
    pz = {j: send(mine_p, mine_p, pz_s.at[j], pz_r.at[j], zs[j]) for j in zs}
    half = pa.at[c, pl.ds(pl.multiple_of(xh * 128, 128), 128), pl.ds(pcol, 512)]
    px = {j: send(half, half, px_s.at[j], px_r.at[j], xs[j]) for j in xs}
    quarter = pa.at[c, :, pl.ds(pl.multiple_of(y * 1024, 1024), 1024)]
    py = {j: send(quarter, quarter, py_s.at[j], py_r.at[j], ys[j]) for j in ys}
    pc = send(pa.at[c], pa.at[c], pc_s, pc_r, peer)
    for j in pz:
        pz[j].start()

    o = owner_ref[0]
    oz, oh, oc = o // 4, lax.rem(o // 2, 2), lax.rem(o, 2)
    here = jnp.logical_and(oz == z, oh == xh)
    mine = jnp.logical_and(here, oc == c)
    other = jnp.logical_and(here, oc == 1 - c)

    def place(core):
        v = lax.rem((z - oz) * (1 - 2 * core) + 8, 8)
        e = lax.rem(oz + xl + core, 2)
        across = (e + lax.rem(v - e + 8, 8)) * L + L2
        return v, e, jnp.where(oh == xh, v * L, across)

    dist = lax.rem((z - oz) * (1 - 2 * c) + 8, 8)
    enter = lax.rem(oz + xl + c, 2)
    use_rung = jnp.logical_and(oh != xh, dist == enter)
    rung = lax.rem(z + xl + c, 2) == 0
    nxt = {"z": lax.rem(z + 9 - 2 * c, 8)}

    def ring(s):
        return send(stream.at[c, s], ring_in.at[s], ring_s.at[s], ring_r.at[s], nxt)

    def cross(s):
        return send(stream.at[c, s], rung_in.at[s], rung_s.at[s], rung_r.at[s], {"xh": 1 - xh})

    def share(b):
        block = stream.at[c, pl.ds(b * BATCH, BATCH)]
        return send(block, block, share_s.at[b], share_r.at[b], peer)

    def step(s, lo):
        from_ring, injecting = lo >= L, lo < N
        from_rung = L2 <= lo < N + L + L2
        if injecting:
            rows = pl.ds(pl.multiple_of(lax.rem(s, 16) * 16, 16), 16)
        if from_ring:
            ring(s - L).wait_recv()

        def content(with_rung):
            value = None
            if from_ring:
                value = ring_in[s - L]
            if with_rung:
                value = jnp.where(use_rung, rung_in[s - L2], value)
            if injecting:
                a, b = own[s // 16, rows, :], oth[s // 16, rows, :]
                rest = b if value is None else jnp.where(other, b, value)
                value = jnp.where(mine, a, rest)
            return value

        if from_rung:

            @pl.when(rung)
            def _():
                cross(s - L2).wait_recv()
                stream[c, s] = content(True)

            @pl.when(jnp.logical_not(rung))
            def _():
                stream[c, s] = content(False)

        else:
            stream[c, s] = content(False)
        if lo < S - L:
            ring(s).start()
        if lo < N + L:

            @pl.when(rung)
            def _():
                cross(s).start()

        @pl.when(lax.rem(s, BATCH) == BATCH - 1)
        def _():
            share(s // BATCH).start()

    def run(a, b):
        cuts = [a] + [k for k in EDGES if a < k < b] + [b]
        for lo, hi in zip(cuts[:-1], cuts[1:]):
            if lo < N and lo % 16 == 0:
                pltpu.make_async_copy(own.at[lo // 16], own.at[lo // 16], own_sem.at[lo // 16]).wait()
                k = lo // 16
                send(oth.at[k], oth.at[k], oth_s.at[k], oth_r.at[k], peer).wait()

            def body(s, carry, lo=lo):
                step(s, lo)
                return carry

            lax.fori_loop(lo, hi, body, 0)

    run(0, 24)
    load_q.start()
    load_t.start()
    for j in pz:
        pz[j].wait_recv()
    for j in px:
        px[j].start()
    run(24, 40)
    for j in px:
        px[j].wait_recv()
    for j in py:
        py[j].start()
    run(40, 116)
    for j in py:
        py[j].wait_recv()
    pc.start()
    run(116, S)
    load_q.wait()
    load_t.wait()
    pc.wait_recv()

    for h in range(2):
        zp_t[pl.ds(h * 256, 256), :] = dot_nt(pa[h], q[...]) * SCALE

    def got_share(b, carry):
        share(b).wait_recv()
        return carry

    lax.fori_loop(0, NB, got_share, 0)
    _, _, at_s = place(0)
    _, _, at_t = place(1)

    def bank(core, at, i):
        return stream[core, pl.ds(at + 16 * i, 16)].reshape(256, CW)

    for target, core, at, left in ((zq_t, 0, at_s, q), (tt_t, 1, at_t, t)):
        for i in range(PARTS):
            part = dot_nt(bank(core, at, i), left[:, pl.ds(i * CW, CW)])
            target[...] = part if i == 0 else target[...] + part
    zq = zq_t[...] * SCALE
    weight = jnp.transpose(keep_ref[...].astype(F32)) * jax.nn.sigmoid(-(tt_t[...] * SCALE))
    zp = zp_t[...]
    top = jnp.maximum(jnp.max(zp, axis=0, keepdims=True), jnp.max(zq, axis=0, keepdims=True))
    total = jnp.sum(jnp.exp(zp - top), axis=0, keepdims=True) + jnp.sum(
        weight * jnp.exp(zq - top), axis=0, keepdims=True
    )
    lse = top + jnp.log(total)
    k = lax.broadcasted_iota(jnp.int32, (512, 512), 0)
    ids = (lax.rem(k // 16, 8) * 4 + lax.rem(k // 128, 2) * 2 + k // 256) * 16 + lax.rem(k, 16)
    hit = (ids == pos_ref[...]).astype(F32)
    loss_ref[...] = lse - jnp.sum(zp * hit, axis=0, keepdims=True)
    grad = jnp.exp(zp - lse) - hit
    gp_t[...] = grad.astype(BF)
    gp[...] = jnp.transpose(grad).astype(BF)
    gq[...] = jnp.transpose(weight * jnp.exp(zq - lse)).astype(BF)

    my_rows = gp_t.at[pl.ds(pl.multiple_of(c * 256, 256), 256), :]
    its_rows = gp_t.at[pl.ds(pl.multiple_of((1 - c) * 256, 256), 256), :]
    order = (2, 1, 3, 0)
    gcs = {}
    for j in order:
        cols = pl.ds(pl.multiple_of(lax.rem(y + j, 4) * 1024, 1024), 1024)
        give[:, cols] = dot(its_rows[...], q[:, cols]).astype(BF)
        gcs[j] = send(give.at[:, cols], got.at[:, cols], gc_s.at[j], gc_r.at[j], peer)
        gcs[j].start()
        kept[:, cols] = dot(my_rows[...], q[:, cols])

    def g1y(j):
        cols = pl.ds(pl.multiple_of(lax.rem(y + j, 4) * 1024, 1024), 1024)
        return cols, send(merged.at[:, cols], first_y.at[j - 1], g1_s.at[j], g1_r.at[j], ys[j])

    def g1x(j):
        there = xs[j]
        rows = pl.ds(pl.multiple_of(there["xh"] * 128, 128), 128)
        cols = pl.ds(pl.multiple_of(there["xl"] * 2048, 2048), 2048)
        return rows, cols, send(
            merged.at[rows, cols], first_x.at[j - 1], g1_s.at[j], g1_r.at[j], xs[j]
        )

    def g2(j, device):
        return send(second_out.at[j - 1], second_in.at[j - 1], g2_s.at[j], g2_r.at[j], device)

    @pl.when(c == 0)
    def _():
        for j in order[:3]:
            gcs[j].wait_recv()
            cols, copy = g1y(j)
            merged[:, cols] = (kept[:, cols] + got[:, cols].astype(F32)).astype(BF)
            copy.start()
        gcs[0].wait_recv()

    @pl.when(c == 1)
    def _():
        for j in order:
            gcs[j].wait_recv()
        for j in order[:3]:
            rows, cols, copy = g1x(j)
            merged[rows, cols] = (kept[rows, cols] + got[rows, cols].astype(F32)).astype(BF)
            copy.start()

    outs = []
    for i in range(PARTS):
        cols = pl.ds(i * CW, CW)
        value = dot(gp[:, :256], pa[0, :, cols]) + dot(gp[:, 256:], pa[1, :, cols])
        value = value + dot(gq[...], bank(0, at_s, i))
        t[:, cols] = (value * SCALE).astype(BF)
        outs.append(pltpu.make_async_copy(t.at[:, cols], qg_hbm.at[:, cols], out_sem.at[i]))
        outs[-1].start()

    @pl.when(c == 0)
    def _():
        for j in order[:3]:
            g1y(j)[1].wait_recv()
        for j in order:
            device = along_x(j)
            rows = pl.ds(pl.multiple_of(device["xh"] * 128, 128), 128)
            low = device["xl"] * 512
            cols = pl.ds(pl.multiple_of(y * 1024 + low, 512), 512)
            inner = pl.ds(pl.multiple_of(low, 512), 512)
            value = kept[rows, cols] + got[rows, cols].astype(F32)
            for k in range(3):
                value = value + first_y[k, rows, inner].astype(F32)
            if j:
                second_out[j - 1] = value.astype(BF)
                g2(j, device).start()
            else:
                piece[...] = value

    @pl.when(c == 1)
    def _():
        for j in order[:3]:
            g1x(j)[2].wait_recv()
        rows = pl.ds(pl.multiple_of(xh * 128, 128), 128)
        for j in order:
            low = lax.rem(y + j, 4) * 512
            cols = pl.ds(pl.multiple_of(xl * 2048 + low, 512), 512)
            inner = pl.ds(pl.multiple_of(low, 512), 512)
            value = kept[rows, cols] + got[rows, cols].astype(F32)
            for k in range(3):
                value = value + first_x[k, :, inner].astype(F32)
            if j:
                second_out[j - 1] = value.astype(BF)
                g2(j, ys[j]).start()
            else:
                piece[...] = value

    for j in order[:3]:
        g2(j, peer).wait_recv()
    piece[...] = piece[...] + (
        second_in[0].astype(F32) + second_in[1].astype(F32) + second_in[2].astype(F32)
    )

    def g3(j):
        rows = pl.ds(pl.multiple_of(lax.rem(z + j, 8) * 16, 16), 16)
        return send(piece.at[rows, :], third_in.at[j - 1], g3_s.at[j], g3_r.at[j], zs[j])

    for j in (4, 3, 5, 2, 6, 1, 7):
        g3(j).start()
    final = piece[pl.ds(pl.multiple_of(z * 16, 16), 16), :]
    for j in (1, 7, 2, 6, 3, 5, 4):
        g3(j).wait_recv()
        final = final + third_in[j - 1]
    col = (1 - c) * (y * 1024 + xl * 512) + c * (xl * 2048 + y * 512)
    part = pg_ref.at[:, pl.ds(pl.multiple_of(col, 512), 512)]
    part[...] = final * SCALE
    g4 = {j: send(part, part, g4_s.at[j], g4_r.at[j], dps[j]) for j in dps}
    for j in g4:
        g4[j].start()

    for j in pz:
        pz[j].wait_send()
    for copies in (px, py, gcs):
        for j in copies:
            copies[j].wait_send()
    pc.wait_send()

    def sent(s, carry):
        ring(s).wait_send()
        return carry

    lax.fori_loop(0, S - L, sent, 0)

    def shared(b, carry):
        share(b).wait_send()
        return carry

    lax.fori_loop(0, NB, shared, 0)

    @pl.when(rung)
    def _():
        def crossed(s, carry):
            cross(s).wait_send()
            return carry

        lax.fori_loop(0, N + L, crossed, 0)

    @pl.when(c == 0)
    def _():
        for j in order[:3]:
            g1y(j)[1].wait_send()

    @pl.when(c == 1)
    def _():
        for j in order[:3]:
            g1x(j)[2].wait_send()

    for j in order[:3]:
        g2(j, peer).wait_send()
    for j in zs:
        g3(j).wait_send()
    for copy in outs:
        copy.wait()
    for j in g4:
        g4[j].wait()


def body(queries, teacher_queries, passages, bank_student, bank_teacher, owner, positives, keep):
    hbm = pl.BlockSpec(memory_space=pl.ANY)
    vmem = pl.BlockSpec(memory_space=pltpu.VMEM)
    dma = pltpu.SemaphoreType.DMA
    loss, query_grad, passage_grad = pl.pallas_call(
        kernel,
        out_shape=(
            jax.ShapeDtypeStruct((1, 512), F32),
            jax.ShapeDtypeStruct((512, E), BF),
            jax.ShapeDtypeStruct((16, E), F32),
        ),
        in_specs=[pl.BlockSpec(memory_space=pltpu.SMEM), hbm, hbm, hbm, hbm, hbm, vmem, vmem],
        out_specs=(vmem, hbm, vmem),
        scratch_shapes=[
            pltpu.VMEM((512, E), BF),
            pltpu.VMEM((512, E), BF),
            pltpu.VMEM((2, 256, E), BF),
            pltpu.VMEM((PARTS, 256, CW), BF),
            pltpu.VMEM((PARTS, 256, CW), BF),
            pltpu.VMEM((S - L, 16, CW), BF),
            pltpu.VMEM((N + L, 16, CW), BF),
            pltpu.VMEM((2, S, 16, CW), BF),
            pltpu.VMEM((512, 512), F32),
            pltpu.VMEM((256, 512), F32),
            pltpu.VMEM((256, 512), F32),
            pltpu.VMEM((512, 512), BF),
            pltpu.VMEM((512, 512), BF),
            pltpu.VMEM((512, 256), BF),
            pltpu.VMEM((256, E), BF),
            pltpu.VMEM((256, E), BF),
            pltpu.VMEM((256, E), F32),
            pltpu.VMEM((256, E), BF),
            pltpu.VMEM((3, 256, 1024), BF),
            pltpu.VMEM((3, 128, 2048), BF),
            pltpu.VMEM((3, 128, 512), BF),
            pltpu.VMEM((3, 128, 512), BF),
            pltpu.VMEM((128, 512), F32),
            pltpu.VMEM((7, 16, 512), F32),
            dma((3,)), dma((PARTS,)), dma((PARTS,)), dma((PARTS,)),
            dma((S - L,)), dma((S - L,)), dma((N + L,)), dma((N + L,)), dma((NB,)), dma((NB,)),
            dma((8,)), dma((8,)), dma((4,)), dma((4,)), dma((4,)), dma((4,)), dma, dma,
            dma((4,)), dma((4,)), dma((4,)), dma((4,)), dma((4,)), dma((4,)),
            dma((8,)), dma((8,)), dma((8,)), dma((8,)), dma((PARTS,)),
        ],
        compiler_params=pltpu.CompilerParams(
            collective_id=0, has_side_effects=True, vmem_limit_bytes=60 << 20
        ),
        name="distill_step",
    )(
        owner, queries, teacher_queries, passages, bank_student, bank_teacher,
        positives.reshape(1, 512), keep,
    )
    return loss.reshape(512), query_grad, passage_grad


def solution(mesh):
    torus = Mesh(mesh.devices.reshape(8, 2, 2, 4, 2), AXES)
    in_specs = (
        P(AXES, None),
        P(AXES, None),
        P(WIDE, None),
        P(WIDE, None),
        P(WIDE, None),
        P(DP),
        P(AXES),
        P(AXES, None),
    )
    out_specs = (P(AXES), P(AXES, None), P(WIDE, None))
    return jax.shard_map(body, mesh=torus, in_specs=in_specs, out_specs=out_specs, check_vma=False)
```

```python
import math

import jax
import jax.numpy as jnp
from jax import lax
from jax.experimental import pallas as pl
from jax.experimental.pallas import tpu as pltpu
from jax.sharding import Mesh
from jax.sharding import PartitionSpec as P

E = 4096
WIDE = ("z", "xh", "c")
DP = ("y", "xl")
AXES = WIDE + DP
MESH = pl.DeviceIdType.MESH
SCALE = 2.0 / math.sqrt(E)
BF = jnp.bfloat16
F32 = jnp.float32

PARTS = 4
CW = E // PARTS
N = PARTS * 16
L = 9
L2 = 12
S = N + 8 * L + L2
BATCH = 4
NB = S // BATCH
assert S % BATCH == 0
EDGES = sorted({0, L, L2, N, N + L, N + L + L2, S - L, S} | {16 * i for i in range(PARTS)})

NT = (((1,), (1,)), ((), ()))


def dot(a, b):
    return jnp.dot(a, b, preferred_element_type=F32)


def dot_nt(a, b):
    return lax.dot_general(a, b, NT, preferred_element_type=F32)


def kernel(
    owner_ref, q_hbm, t_hbm, p_hbm, bs_hbm, bt_hbm, pos_ref, keep_hbm,
    loss_ref, qg_hbm, pg_ref,
    q, t, keep_ref, pa, own, oth, ring_in, rung_in, stream,
    zp_t, zq_t, tt_t, gp_t, gp, gq,
    give, got, kept, merged, first_y, first_x, second_out, second_in, piece, third_out, third_in,
    load_sem, own_sem, oth_s, oth_r, ring_s, ring_r, rung_s, rung_r, share_s, share_r,
    pz_s, pz_r, px_s, px_r, py_s, py_r, pc_s, pc_r,
    gc_s, gc_r, g1_s, g1_r, g2_s, g2_r, g3_s, g3_r, g4_s, g4_r, out_sem,
):
    z, xh, c, y, xl = [lax.axis_index(a) for a in AXES]
    x = xh * 2 + xl

    def along_x(j):
        other = lax.rem(x + j, 4)
        return {"xh": other // 2, "xl": lax.rem(other, 2)}

    zs = {j: {"z": lax.rem(z + j, 8)} for j in range(1, 8)}
    xs = {j: along_x(j) for j in range(1, 4)}
    ys = {j: {"y": lax.rem(y + j, 4)} for j in range(1, 4)}
    peer = {"c": 1 - c}
    dps = {
        2 * a + b: {"y": lax.rem(y + a, 4), "xl": lax.rem(xl + b, 2)}
        for a in range(4)
        for b in range(2)
        if a or b
    }

    def send(src, dst, send_sem, recv_sem, device):
        return pltpu.make_async_remote_copy(
            src, dst, send_sem, recv_sem, device_id=device, device_id_type=MESH
        )

    barrier = pltpu.get_barrier_semaphore()
    greeted = [*zs.values(), *xs.values(), peer, *[dps[k] for k in dps if k != 1]]
    for device in greeted:
        pl.semaphore_signal(barrier, inc=1, device_id=device, device_id_type=MESH)

    pcol = pl.multiple_of(y * 1024 + xl * 512, 512)
    prow = pl.multiple_of(xh * 128 + z * 16, 16)
    mine_p = pa.at[c, pl.ds(prow, 16), pl.ds(pcol, 512)]
    load_p = pltpu.make_async_copy(p_hbm.at[:, pl.ds(pcol, 512)], mine_p, load_sem.at[2])
    load_p.start()

    def own_loads(src):
        return [
            pltpu.make_async_copy(src.at[:, pl.ds(i * CW, CW)], own.at[i], own_sem.at[i])
            for i in range(PARTS)
        ]

    def other_loads(src):
        return [
            send(src.at[:, pl.ds(i * CW, CW)], oth.at[i], oth_s.at[i], oth_r.at[i], peer)
            for i in range(PARTS)
        ]

    @pl.when(c == 0)
    def _():
        for k in own_loads(bs_hbm):
            k.start()

    @pl.when(c == 1)
    def _():
        for k in own_loads(bt_hbm):
            k.start()

    load_q = pltpu.make_async_copy(q_hbm, q, load_sem.at[0])
    load_t = pltpu.make_async_copy(t_hbm, t, load_sem.at[1])
    load_keep = pltpu.make_async_copy(keep_hbm, keep_ref, load_sem.at[3])
    pl.semaphore_wait(barrier, len(greeted))

    @pl.when(c == 0)
    def _():
        for k in other_loads(bt_hbm):
            k.start()

    @pl.when(c == 1)
    def _():
        for k in other_loads(bs_hbm):
            k.start()

    load_p.wait()
    pz = {j: send(mine_p, mine_p, pz_s.at[j], pz_r.at[j], zs[j]) for j in zs}
    half = pa.at[c, pl.ds(pl.multiple_of(xh * 128, 128), 128), pl.ds(pcol, 512)]
    px = {j: send(half, half, px_s.at[j], px_r.at[j], xs[j]) for j in xs}
    quarter = pa.at[c, :, pl.ds(pl.multiple_of(y * 1024, 1024), 1024)]
    py = {j: send(quarter, quarter, py_s.at[j], py_r.at[j], ys[j]) for j in ys}
    pc = send(pa.at[c], pa.at[c], pc_s, pc_r, peer)
    for j in pz:
        pz[j].start()

    o = owner_ref[0]
    oz, oh, oc = o // 4, lax.rem(o // 2, 2), lax.rem(o, 2)
    here = jnp.logical_and(oz == z, oh == xh)
    mine = jnp.logical_and(here, oc == c)
    other = jnp.logical_and(here, oc == 1 - c)

    def place(core):
        v = lax.rem((z - oz) * (1 - 2 * core) + 8, 8)
        e = lax.rem(oz + xl + core, 2)
        across = (e + lax.rem(v - e + 8, 8)) * L + L2
        return v, e, jnp.where(oh == xh, v * L, across)

    dist = lax.rem((z - oz) * (1 - 2 * c) + 8, 8)
    enter = lax.rem(oz + xl + c, 2)
    use_rung = jnp.logical_and(oh != xh, dist == enter)
    rung = lax.rem(z + xl + c, 2) == 0
    nxt = {"z": lax.rem(z + 9 - 2 * c, 8)}

    def ring(s):
        return send(stream.at[c, s], ring_in.at[s], ring_s.at[s], ring_r.at[s], nxt)

    def cross(s):
        return send(stream.at[c, s], rung_in.at[s], rung_s.at[s], rung_r.at[s], {"xh": 1 - xh})

    def share(b):
        block = stream.at[c, pl.ds(b * BATCH, BATCH)]
        return send(block, block, share_s.at[b], share_r.at[b], peer)

    def step(s, lo):
        from_ring, injecting = lo >= L, lo < N
        from_rung = L2 <= lo < N + L + L2
        if injecting:
            rows = pl.ds(pl.multiple_of(lax.rem(s, 16) * 16, 16), 16)
        if from_ring:
            ring(s - L).wait_recv()

        def content(with_rung):
            value = None
            if from_ring:
                value = ring_in[s - L]
            if with_rung:
                value = jnp.where(use_rung, rung_in[s - L2], value)
            if injecting:
                a, b = own[s // 16, rows, :], oth[s // 16, rows, :]
                rest = b if value is None else jnp.where(other, b, value)
                value = jnp.where(mine, a, rest)
            return value

        if from_rung:

            @pl.when(rung)
            def _():
                cross(s - L2).wait_recv()
                stream[c, s] = content(True)

            @pl.when(jnp.logical_not(rung))
            def _():
                stream[c, s] = content(False)

        else:
            stream[c, s] = content(False)
        if lo < S - L:
            ring(s).start()
        if lo < N + L:

            @pl.when(rung)
            def _():
                cross(s).start()

        @pl.when(lax.rem(s, BATCH) == BATCH - 1)
        def _():
            share(s // BATCH).start()

    def run(a, b):
        cuts = [a] + [k for k in EDGES if a < k < b] + [b]
        for lo, hi in zip(cuts[:-1], cuts[1:]):
            if lo < N and lo % 16 == 0:
                pltpu.make_async_copy(own.at[lo // 16], own.at[lo // 16], own_sem.at[lo // 16]).wait()
                k = lo // 16
                send(oth.at[k], oth.at[k], oth_s.at[k], oth_r.at[k], peer).wait()

            def body(s, carry, lo=lo):
                step(s, lo)
                return carry

            lax.fori_loop(lo, hi, body, 0)

    run(0, 24)
    load_q.start()
    load_t.start()
    load_keep.start()
    for j in pz:
        pz[j].wait_recv()
    for j in px:
        px[j].start()
    run(24, 40)
    for j in px:
        px[j].wait_recv()
    for j in py:
        py[j].start()
    run(40, 116)
    for j in py:
        py[j].wait_recv()
    pc.start()
    run(116, S)
    load_q.wait()
    load_t.wait()
    load_keep.wait()
    pc.wait_recv()

    for h in range(2):
        zp_t[pl.ds(h * 256, 256), :] = dot_nt(pa[h], q[...]) * SCALE

    def got_share(b, carry):
        share(b).wait_recv()
        return carry

    lax.fori_loop(0, NB, got_share, 0)
    _, _, at_s = place(0)
    _, _, at_t = place(1)

    def bank(core, at, i):
        return stream[core, pl.ds(at + 16 * i, 16)].reshape(256, CW)

    for target, core, at, left in ((zq_t, 0, at_s, q), (tt_t, 1, at_t, t)):
        for i in range(PARTS):
            part = dot_nt(bank(core, at, i), left[:, pl.ds(i * CW, CW)])
            target[...] = part if i == 0 else target[...] + part
    zq = zq_t[...] * SCALE
    weight = jnp.transpose(keep_ref[...].astype(F32)) * jax.nn.sigmoid(-(tt_t[...] * SCALE))
    zp = zp_t[...]
    top = jnp.maximum(jnp.max(zp, axis=0, keepdims=True), jnp.max(zq, axis=0, keepdims=True))
    total = jnp.sum(jnp.exp(zp - top), axis=0, keepdims=True) + jnp.sum(
        weight * jnp.exp(zq - top), axis=0, keepdims=True
    )
    lse = top + jnp.log(total)
    k = lax.broadcasted_iota(jnp.int32, (512, 512), 0)
    ids = (lax.rem(k // 16, 8) * 4 + lax.rem(k // 128, 2) * 2 + k // 256) * 16 + lax.rem(k, 16)
    hit = (ids == pos_ref[...]).astype(F32)
    loss = lse - jnp.sum(zp * hit, axis=0, keepdims=True)
    for i in range(4):
        loss_ref[pl.ds(i, 1), :] = loss[:, i * 128 : (i + 1) * 128]
    grad = jnp.exp(zp - lse) - hit
    gp_t[...] = grad.astype(BF)
    gp[...] = jnp.transpose(grad).astype(BF)
    gq[...] = jnp.transpose(weight * jnp.exp(zq - lse)).astype(BF)

    my_rows = gp_t.at[pl.ds(pl.multiple_of(c * 256, 256), 256), :]
    its_rows = gp_t.at[pl.ds(pl.multiple_of((1 - c) * 256, 256), 256), :]
    order = (2, 1, 3, 0)
    y_cols = [lax.rem(y + j, 4) * 1024 for j in order]
    x_cols = [((1 - xl) * 2 + i) * 1024 for i in range(2)] + [(xl * 2 + i) * 1024 for i in range(2)]
    gcs = []
    for i in range(4):
        for_it = pl.multiple_of(c * y_cols[i] + (1 - c) * x_cols[i], 1024)
        for_me = pl.multiple_of((1 - c) * y_cols[i] + c * x_cols[i], 1024)
        give[:, pl.ds(for_it, 1024)] = dot(its_rows[...], q[:, pl.ds(for_it, 1024)]).astype(BF)
        there = give.at[:, pl.ds(for_it, 1024)]
        gcs.append(send(there, got.at[:, pl.ds(for_it, 1024)], gc_s.at[i], gc_r.at[i], peer))
        gcs[-1].start()
        kept[:, pl.ds(for_me, 1024)] = dot(my_rows[...], q[:, pl.ds(for_me, 1024)])

    def g1y(j):
        cols = pl.ds(pl.multiple_of(lax.rem(y + j, 4) * 1024, 1024), 1024)
        return cols, send(merged.at[:, cols], first_y.at[j - 1], g1_s.at[j], g1_r.at[j], ys[j])

    def g1x(j):
        there = xs[j]
        rows = pl.ds(pl.multiple_of(there["xh"] * 128, 128), 128)
        cols = pl.ds(pl.multiple_of(there["xl"] * 2048, 2048), 2048)
        return rows, cols, send(
            merged.at[rows, cols], first_x.at[j - 1], g1_s.at[j], g1_r.at[j], xs[j]
        )

    def g2(j, device):
        return send(second_out.at[j - 1], second_in.at[j - 1], g2_s.at[j], g2_r.at[j], device)

    @pl.when(c == 0)
    def _():
        for i, j in enumerate(order[:3]):
            gcs[i].wait_recv()
            cols, copy = g1y(j)
            merged[:, cols] = (kept[:, cols] + got[:, cols].astype(F32)).astype(BF)
            copy.start()
        gcs[3].wait_recv()

    @pl.when(c == 1)
    def _():
        for j in (1, 3, 2):
            if j != 3:
                for i in (0, 1) if j == 1 else (2, 3):
                    gcs[i].wait_recv()
            rows, cols, copy = g1x(j)
            merged[rows, cols] = (kept[rows, cols] + got[rows, cols].astype(F32)).astype(BF)
            copy.start()

    outs = []
    for i in range(PARTS):
        cols = pl.ds(i * CW, CW)
        value = dot(gp[:, :256], pa[0, :, cols]) + dot(gp[:, 256:], pa[1, :, cols])
        value = value + dot(gq[...], bank(0, at_s, i))
        t[:, cols] = (value * SCALE).astype(BF)
        outs.append(pltpu.make_async_copy(t.at[:, cols], qg_hbm.at[:, cols], out_sem.at[i]))
        outs[-1].start()

    for j in pz:
        pz[j].wait_send()
    for copies in (px, py):
        for j in copies:
            copies[j].wait_send()
    pc.wait_send()
    for copy in gcs:
        copy.wait_send()

    def sent(s, carry):
        ring(s).wait_send()
        return carry

    lax.fori_loop(0, S - L, sent, 0)

    def shared(b, carry):
        share(b).wait_send()
        return carry

    lax.fori_loop(0, NB, shared, 0)

    @pl.when(rung)
    def _():
        def crossed(s, carry):
            cross(s).wait_send()
            return carry

        lax.fori_loop(0, N + L, crossed, 0)

    @pl.when(c == 0)
    def _():
        for j in order[:3]:
            g1y(j)[1].wait_recv()
        for j in order:
            device = along_x(j)
            rows = pl.ds(pl.multiple_of(device["xh"] * 128, 128), 128)
            low = device["xl"] * 512
            cols = pl.ds(pl.multiple_of(y * 1024 + low, 512), 512)
            inner = pl.ds(pl.multiple_of(low, 512), 512)
            value = kept[rows, cols] + got[rows, cols].astype(F32)
            for k in range(3):
                value = value + first_y[k, rows, inner].astype(F32)
            if j:
                second_out[j - 1] = value.astype(BF)
                g2(j, device).start()
            else:
                piece[...] = value

    @pl.when(c == 1)
    def _():
        for j in order[:3]:
            g1x(j)[2].wait_recv()
        rows = pl.ds(pl.multiple_of(xh * 128, 128), 128)
        for j in order:
            low = lax.rem(y + j, 4) * 512
            cols = pl.ds(pl.multiple_of(xl * 2048 + low, 512), 512)
            inner = pl.ds(pl.multiple_of(low, 512), 512)
            value = kept[rows, cols] + got[rows, cols].astype(F32)
            for k in range(3):
                value = value + first_x[k, :, inner].astype(F32)
            if j:
                second_out[j - 1] = value.astype(BF)
                g2(j, ys[j]).start()
            else:
                piece[...] = value

    for j in order[:3]:
        g2(j, peer).wait_recv()
    piece[...] = piece[...] + (
        second_in[0].astype(F32) + second_in[1].astype(F32) + second_in[2].astype(F32)
    )

    third_out[...] = piece[...].astype(BF)

    def g3(j):
        rows = pl.ds(pl.multiple_of(lax.rem(z + j, 8) * 16, 16), 16)
        return send(third_out.at[rows, :], third_in.at[j - 1], g3_s.at[j], g3_r.at[j], zs[j])

    for j in (4, 3, 5, 2, 6, 1, 7):
        g3(j).start()
    final = piece[pl.ds(pl.multiple_of(z * 16, 16), 16), :]
    for j in (1, 7, 2, 6, 3, 5, 4):
        g3(j).wait_recv()
        final = final + third_in[j - 1].astype(F32)
    col = (1 - c) * (y * 1024 + xl * 512) + c * (xl * 2048 + y * 512)
    part = pg_ref.at[:, pl.ds(pl.multiple_of(col, 512), 512)]
    part[...] = final * SCALE
    g4 = {j: send(part, part, g4_s.at[j], g4_r.at[j], dps[j]) for j in dps}
    for j in g4:
        g4[j].start()

    @pl.when(c == 0)
    def _():
        for j in order[:3]:
            g1y(j)[1].wait_send()

    @pl.when(c == 1)
    def _():
        for j in order[:3]:
            g1x(j)[2].wait_send()

    for j in order[:3]:
        g2(j, peer).wait_send()
    for j in zs:
        g3(j).wait_send()
    for copy in outs:
        copy.wait()
    for j in g4:
        g4[j].wait()


def body(queries, teacher_queries, passages, bank_student, bank_teacher, owner, positives, keep):
    hbm = pl.BlockSpec(memory_space=pl.ANY)
    vmem = pl.BlockSpec(memory_space=pltpu.VMEM)
    dma = pltpu.SemaphoreType.DMA
    loss, query_grad, passage_grad = pl.pallas_call(
        kernel,
        out_shape=(
            jax.ShapeDtypeStruct((4, 128), F32),
            jax.ShapeDtypeStruct((512, E), BF),
            jax.ShapeDtypeStruct((16, E), F32),
        ),
        in_specs=[pl.BlockSpec(memory_space=pltpu.SMEM), hbm, hbm, hbm, hbm, hbm, vmem, hbm],
        out_specs=(vmem, hbm, vmem),
        scratch_shapes=[
            pltpu.VMEM((512, E), BF),
            pltpu.VMEM((512, E), BF),
            pltpu.VMEM((512, 256), jnp.int32),
            pltpu.VMEM((2, 256, E), BF),
            pltpu.VMEM((PARTS, 256, CW), BF),
            pltpu.VMEM((PARTS, 256, CW), BF),
            pltpu.VMEM((S - L, 16, CW), BF),
            pltpu.VMEM((N + L, 16, CW), BF),
            pltpu.VMEM((2, S, 16, CW), BF),
            pltpu.VMEM((512, 512), F32),
            pltpu.VMEM((256, 512), F32),
            pltpu.VMEM((256, 512), F32),
            pltpu.VMEM((512, 512), BF),
            pltpu.VMEM((512, 512), BF),
            pltpu.VMEM((512, 256), BF),
            pltpu.VMEM((256, E), BF),
            pltpu.VMEM((256, E), BF),
            pltpu.VMEM((256, E), F32),
            pltpu.VMEM((256, E), BF),
            pltpu.VMEM((3, 256, 1024), BF),
            pltpu.VMEM((3, 128, 2048), BF),
            pltpu.VMEM((3, 128, 512), BF),
            pltpu.VMEM((3, 128, 512), BF),
            pltpu.VMEM((128, 512), F32),
            pltpu.VMEM((128, 512), BF),
            pltpu.VMEM((7, 16, 512), BF),
            dma((4,)), dma((PARTS,)), dma((PARTS,)), dma((PARTS,)),
            dma((S - L,)), dma((S - L,)), dma((N + L,)), dma((N + L,)), dma((NB,)), dma((NB,)),
            dma((8,)), dma((8,)), dma((4,)), dma((4,)), dma((4,)), dma((4,)), dma, dma,
            dma((4,)), dma((4,)), dma((4,)), dma((4,)), dma((4,)), dma((4,)),
            dma((8,)), dma((8,)), dma((8,)), dma((8,)), dma((PARTS,)),
        ],
        compiler_params=pltpu.CompilerParams(
            collective_id=0, has_side_effects=True, vmem_limit_bytes=60 << 20
        ),
        name="distill_step",
    )(
        owner, queries, teacher_queries, passages, bank_student, bank_teacher,
        positives.reshape(1, 512), keep,
    )
    return loss.reshape(512), query_grad, passage_grad


def solution(mesh):
    torus = Mesh(mesh.devices.reshape(8, 2, 2, 4, 2), AXES)
    in_specs = (
        P(AXES, None),
        P(AXES, None),
        P(WIDE, None),
        P(WIDE, None),
        P(WIDE, None),
        P(DP),
        P(AXES),
        P(AXES, None),
    )
    out_specs = (P(AXES), P(AXES, None), P(WIDE, None))
    return jax.shard_map(body, mesh=torus, in_specs=in_specs, out_specs=out_specs, check_vma=False)
```

```python
import math

import jax
import jax.numpy as jnp
from jax import lax
from jax.experimental import pallas as pl
from jax.experimental.pallas import tpu as pltpu
from jax.sharding import Mesh
from jax.sharding import PartitionSpec as P

E = 4096
WIDE = ("z", "xh", "c")
DP = ("y", "xl")
AXES = WIDE + DP
MESH = pl.DeviceIdType.MESH
SCALE = 2.0 / math.sqrt(E)
BF = jnp.bfloat16
F32 = jnp.float32

PARTS = 4
CW = E // PARTS
PIECES = PARTS + 1
ONE_WAY = 16 * (PARTS - 1)
N = 16 * PIECES
L = 8
L2 = 12
S = max(ONE_WAY + 8 * L, N + 4 * L) + L2
BATCH = 4
NB = S // BATCH
assert S % BATCH == 0
EDGES = sorted({0, L, L2, N, N + L, N + L + L2, S - L, S} | {16 * i for i in range(PIECES)})

NT = (((1,), (1,)), ((), ()))


def dot(a, b):
    return jnp.dot(a, b, preferred_element_type=F32)


def dot_nt(a, b):
    return lax.dot_general(a, b, NT, preferred_element_type=F32)


def kernel(
    owner_ref, q_hbm, t_hbm, p_hbm, bs_hbm, bt_hbm, pos_ref, keep_hbm,
    loss_ref, qg_hbm, pg_ref,
    q, t, keep_ref, pa, own, oth, ring_in, rung_in, stream,
    zp_t, zq_t, tt_t, gp_t, gp, gq,
    give, got, kept, merged, first_y, first_x, second_out, second_in, piece, third_out, third_in,
    load_sem, own_sem, oth_s, oth_r, ring_s, ring_r, rung_s, rung_r, share_s, share_r,
    pz_s, pz_r, px_s, px_r, py_s, py_r, pc_s, pc_r,
    gc_s, gc_r, g1_s, g1_r, g2_s, g2_r, g3_s, g3_r, g4_s, g4_r, out_sem,
):
    z, xh, c, y, xl = [lax.axis_index(a) for a in AXES]
    x = xh * 2 + xl

    def along_x(j):
        other = lax.rem(x + j, 4)
        return {"xh": other // 2, "xl": lax.rem(other, 2)}

    zs = {j: {"z": lax.rem(z + j, 8)} for j in range(1, 8)}
    xs = {j: along_x(j) for j in range(1, 4)}
    ys = {j: {"y": lax.rem(y + j, 4)} for j in range(1, 4)}
    peer = {"c": 1 - c}
    dps = {
        2 * a + b: {"y": lax.rem(y + a, 4), "xl": lax.rem(xl + b, 2)}
        for a in range(4)
        for b in range(2)
        if a or b
    }

    def send(src, dst, send_sem, recv_sem, device):
        return pltpu.make_async_remote_copy(
            src, dst, send_sem, recv_sem, device_id=device, device_id_type=MESH
        )

    barrier = pltpu.get_barrier_semaphore()
    greeted = [*zs.values(), *xs.values(), peer, *[dps[k] for k in dps if k != 1]]
    for device in greeted:
        pl.semaphore_signal(barrier, inc=1, device_id=device, device_id_type=MESH)

    pcol = pl.multiple_of(y * 1024 + xl * 512, 512)
    prow = pl.multiple_of(xh * 128 + z * 16, 16)
    mine_p = pa.at[c, pl.ds(prow, 16), pl.ds(pcol, 512)]
    load_p = pltpu.make_async_copy(p_hbm.at[:, pl.ds(pcol, 512)], mine_p, load_sem.at[2])
    load_p.start()

    def pieces(bank):
        last = PARTS - 1
        return [(bank, i) for i in range(last)] + [(bs_hbm, last), (bt_hbm, last)]

    def own_loads(bank):
        return [
            pltpu.make_async_copy(src.at[:, pl.ds(i * CW, CW)], own.at[k], own_sem.at[k])
            for k, (src, i) in enumerate(pieces(bank))
        ]

    def other_loads(bank):
        return [
            send(src.at[:, pl.ds(i * CW, CW)], oth.at[k], oth_s.at[k], oth_r.at[k], peer)
            for k, (src, i) in enumerate(pieces(bank))
        ]

    @pl.when(c == 0)
    def _():
        for k in own_loads(bs_hbm):
            k.start()

    @pl.when(c == 1)
    def _():
        for k in own_loads(bt_hbm):
            k.start()

    load_q = pltpu.make_async_copy(q_hbm, q, load_sem.at[0])
    load_t = pltpu.make_async_copy(t_hbm, t, load_sem.at[1])
    load_keep = pltpu.make_async_copy(keep_hbm, keep_ref, load_sem.at[3])
    pl.semaphore_wait(barrier, len(greeted))

    @pl.when(c == 0)
    def _():
        for k in other_loads(bt_hbm):
            k.start()

    @pl.when(c == 1)
    def _():
        for k in other_loads(bs_hbm):
            k.start()

    load_p.wait()
    pz = {j: send(mine_p, mine_p, pz_s.at[j], pz_r.at[j], zs[j]) for j in zs}
    half = pa.at[c, pl.ds(pl.multiple_of(xh * 128, 128), 128), pl.ds(pcol, 512)]
    px = {j: send(half, half, px_s.at[j], px_r.at[j], xs[j]) for j in xs}
    quarter = pa.at[c, :, pl.ds(pl.multiple_of(y * 1024, 1024), 1024)]
    py = {j: send(quarter, quarter, py_s.at[j], py_r.at[j], ys[j]) for j in ys}
    pc = send(pa.at[c], pa.at[c], pc_s, pc_r, peer)
    for j in pz:
        pz[j].start()

    o = owner_ref[0]
    oz, oh, oc = o // 4, lax.rem(o // 2, 2), lax.rem(o, 2)
    here = jnp.logical_and(oz == z, oh == xh)
    mine = jnp.logical_and(here, oc == c)
    other = jnp.logical_and(here, oc == 1 - c)

    def place(core):
        v = lax.rem((z - oz) * (1 - 2 * core) + 8, 8)
        e = lax.rem(oz + xl + core, 2)
        across = (e + lax.rem(v - e + 8, 8)) * L + L2
        return v, e, jnp.where(oh == xh, v * L, across)

    dist = lax.rem((z - oz) * (1 - 2 * c) + 8, 8)
    enter = lax.rem(oz + xl + c, 2)
    use_rung = jnp.logical_and(oh != xh, dist == enter)
    rung = lax.rem(z + xl + c, 2) == 0
    nxt = {"z": lax.rem(z + 9 - 2 * c, 8)}

    def ring(s):
        return send(stream.at[c, s], ring_in.at[s], ring_s.at[s], ring_r.at[s], nxt)

    def cross(s):
        return send(stream.at[c, s], rung_in.at[s], rung_s.at[s], rung_r.at[s], {"xh": 1 - xh})

    def share(b):
        block = stream.at[c, pl.ds(b * BATCH, BATCH)]
        return send(block, block, share_s.at[b], share_r.at[b], peer)

    def step(s, lo):
        from_ring, injecting = lo >= L, lo < N
        from_rung = L2 <= lo < N + L + L2
        if injecting:
            rows = pl.ds(pl.multiple_of(lax.rem(s, 16) * 16, 16), 16)
        if from_ring:
            ring(s - L).wait_recv()

        def content(with_rung):
            value = None
            if from_ring:
                value = ring_in[s - L]
            if with_rung:
                value = jnp.where(use_rung, rung_in[s - L2], value)
            if injecting:
                a, b = own[s // 16, rows, :], oth[s // 16, rows, :]
                rest = b if value is None else jnp.where(other, b, value)
                value = jnp.where(mine, a, rest)
            return value

        if from_rung:

            @pl.when(rung)
            def _():
                cross(s - L2).wait_recv()
                stream[c, s] = content(True)

            @pl.when(jnp.logical_not(rung))
            def _():
                stream[c, s] = content(False)

        else:
            stream[c, s] = content(False)
        if lo < S - L:
            ring(s).start()
        if lo < N + L:

            @pl.when(rung)
            def _():
                cross(s).start()

        @pl.when(lax.rem(s, BATCH) == BATCH - 1)
        def _():
            share(s // BATCH).start()

    def run(a, b):
        cuts = [a] + [k for k in EDGES if a < k < b] + [b]
        for lo, hi in zip(cuts[:-1], cuts[1:]):
            if lo < N and lo % 16 == 0:
                pltpu.make_async_copy(own.at[lo // 16], own.at[lo // 16], own_sem.at[lo // 16]).wait()
                k = lo // 16
                send(oth.at[k], oth.at[k], oth_s.at[k], oth_r.at[k], peer).wait()

            def body(s, carry, lo=lo):
                step(s, lo)
                return carry

            lax.fori_loop(lo, hi, body, 0)

    run(0, 24)
    load_q.start()
    load_t.start()
    load_keep.start()
    for j in pz:
        pz[j].wait_recv()
    for j in px:
        px[j].start()
    run(24, 40)
    for j in px:
        px[j].wait_recv()
    for j in py:
        py[j].start()
    run(40, 104)
    for j in py:
        py[j].wait_recv()
    pc.start()
    run(104, S)
    load_q.wait()
    load_t.wait()
    load_keep.wait()
    pc.wait_recv()

    for h in range(2):
        zp_t[pl.ds(h * 256, 256), :] = dot_nt(pa[h], q[...]) * SCALE

    def got_share(b, carry):
        share(b).wait_recv()
        return carry

    lax.fori_loop(0, NB, got_share, 0)
    at = [place(0)[2], place(1)[2]]
    nearer = jnp.where(at[0] <= at[1], 0, 1)
    at_last = jnp.minimum(at[0], at[1]) + ONE_WAY

    def bank(array, i):
        if i < PARTS - 1:
            rows = stream[array, pl.ds(at[array] + 16 * i, 16)]
        else:
            rows = stream[nearer, pl.ds(at_last + 16 * array, 16)]
        return rows.reshape(256, CW)

    for target, array, left in ((zq_t, 0, q), (tt_t, 1, t)):
        for i in range(PARTS):
            part = dot_nt(bank(array, i), left[:, pl.ds(i * CW, CW)])
            target[...] = part if i == 0 else target[...] + part
    zq = zq_t[...] * SCALE
    weight = jnp.transpose(keep_ref[...].astype(F32)) * jax.nn.sigmoid(-(tt_t[...] * SCALE))
    zp = zp_t[...]
    top = jnp.maximum(jnp.max(zp, axis=0, keepdims=True), jnp.max(zq, axis=0, keepdims=True))
    total = jnp.sum(jnp.exp(zp - top), axis=0, keepdims=True) + jnp.sum(
        weight * jnp.exp(zq - top), axis=0, keepdims=True
    )
    lse = top + jnp.log(total)
    k = lax.broadcasted_iota(jnp.int32, (512, 512), 0)
    ids = (lax.rem(k // 16, 8) * 4 + lax.rem(k // 128, 2) * 2 + k // 256) * 16 + lax.rem(k, 16)
    hit = (ids == pos_ref[...]).astype(F32)
    loss = lse - jnp.sum(zp * hit, axis=0, keepdims=True)
    for i in range(4):
        loss_ref[pl.ds(i, 1), :] = loss[:, i * 128 : (i + 1) * 128]
    grad = jnp.exp(zp - lse) - hit
    gp_t[...] = grad.astype(BF)
    gp[...] = jnp.transpose(grad).astype(BF)
    gq[...] = jnp.transpose(weight * jnp.exp(zq - lse)).astype(BF)

    my_rows = gp_t.at[pl.ds(pl.multiple_of(c * 256, 256), 256), :]
    its_rows = gp_t.at[pl.ds(pl.multiple_of((1 - c) * 256, 256), 256), :]
    order = (2, 1, 3, 0)
    y_cols = [lax.rem(y + j, 4) * 1024 for j in order]
    x_cols = [((1 - xl) * 2 + i) * 1024 for i in range(2)] + [(xl * 2 + i) * 1024 for i in range(2)]
    gcs = []
    for i in range(4):
        for_it = pl.multiple_of(c * y_cols[i] + (1 - c) * x_cols[i], 1024)
        for_me = pl.multiple_of((1 - c) * y_cols[i] + c * x_cols[i], 1024)
        give[:, pl.ds(for_it, 1024)] = dot(its_rows[...], q[:, pl.ds(for_it, 1024)]).astype(BF)
        there = give.at[:, pl.ds(for_it, 1024)]
        gcs.append(send(there, got.at[:, pl.ds(for_it, 1024)], gc_s.at[i], gc_r.at[i], peer))
        gcs[-1].start()
        kept[:, pl.ds(for_me, 1024)] = dot(my_rows[...], q[:, pl.ds(for_me, 1024)])

    def g1y(j):
        cols = pl.ds(pl.multiple_of(lax.rem(y + j, 4) * 1024, 1024), 1024)
        return cols, send(merged.at[:, cols], first_y.at[j - 1], g1_s.at[j], g1_r.at[j], ys[j])

    def g1x(j):
        there = xs[j]
        rows = pl.ds(pl.multiple_of(there["xh"] * 128, 128), 128)
        cols = pl.ds(pl.multiple_of(there["xl"] * 2048, 2048), 2048)
        return rows, cols, send(
            merged.at[rows, cols], first_x.at[j - 1], g1_s.at[j], g1_r.at[j], xs[j]
        )

    def g2(j, device):
        return send(second_out.at[j - 1], second_in.at[j - 1], g2_s.at[j], g2_r.at[j], device)

    @pl.when(c == 0)
    def _():
        for i, j in enumerate(order[:3]):
            gcs[i].wait_recv()
            cols, copy = g1y(j)
            merged[:, cols] = (kept[:, cols] + got[:, cols].astype(F32)).astype(BF)
            copy.start()
        gcs[3].wait_recv()

    @pl.when(c == 1)
    def _():
        for j in (1, 3, 2):
            if j != 3:
                for i in (0, 1) if j == 1 else (2, 3):
                    gcs[i].wait_recv()
            rows, cols, copy = g1x(j)
            merged[rows, cols] = (kept[rows, cols] + got[rows, cols].astype(F32)).astype(BF)
            copy.start()

    outs = []
    for i in range(PARTS):
        cols = pl.ds(i * CW, CW)
        value = dot(gp[:, :256], pa[0, :, cols]) + dot(gp[:, 256:], pa[1, :, cols])
        value = value + dot(gq[...], bank(0, i))
        t[:, cols] = (value * SCALE).astype(BF)
        outs.append(pltpu.make_async_copy(t.at[:, cols], qg_hbm.at[:, cols], out_sem.at[i]))
        outs[-1].start()

    for j in pz:
        pz[j].wait_send()
    for copies in (px, py):
        for j in copies:
            copies[j].wait_send()
    pc.wait_send()
    for copy in gcs:
        copy.wait_send()

    def sent(s, carry):
        ring(s).wait_send()
        return carry

    lax.fori_loop(0, S - L, sent, 0)

    def shared(b, carry):
        share(b).wait_send()
        return carry

    lax.fori_loop(0, NB, shared, 0)

    @pl.when(rung)
    def _():
        def crossed(s, carry):
            cross(s).wait_send()
            return carry

        lax.fori_loop(0, N + L, crossed, 0)

    @pl.when(c == 0)
    def _():
        for j in order[:3]:
            g1y(j)[1].wait_recv()
        for j in order:
            device = along_x(j)
            rows = pl.ds(pl.multiple_of(device["xh"] * 128, 128), 128)
            low = device["xl"] * 512
            cols = pl.ds(pl.multiple_of(y * 1024 + low, 512), 512)
            inner = pl.ds(pl.multiple_of(low, 512), 512)
            value = kept[rows, cols] + got[rows, cols].astype(F32)
            for k in range(3):
                value = value + first_y[k, rows, inner].astype(F32)
            if j:
                second_out[j - 1] = value.astype(BF)
                g2(j, device).start()
            else:
                piece[...] = value

    @pl.when(c == 1)
    def _():
        for j in order[:3]:
            g1x(j)[2].wait_recv()
        rows = pl.ds(pl.multiple_of(xh * 128, 128), 128)
        for j in order:
            low = lax.rem(y + j, 4) * 512
            cols = pl.ds(pl.multiple_of(xl * 2048 + low, 512), 512)
            inner = pl.ds(pl.multiple_of(low, 512), 512)
            value = kept[rows, cols] + got[rows, cols].astype(F32)
            for k in range(3):
                value = value + first_x[k, :, inner].astype(F32)
            if j:
                second_out[j - 1] = value.astype(BF)
                g2(j, ys[j]).start()
            else:
                piece[...] = value

    for j in order[:3]:
        g2(j, peer).wait_recv()
    piece[...] = piece[...] + (
        second_in[0].astype(F32) + second_in[1].astype(F32) + second_in[2].astype(F32)
    )

    third_out[...] = piece[...].astype(BF)

    def g3(j):
        rows = pl.ds(pl.multiple_of(lax.rem(z + j, 8) * 16, 16), 16)
        return send(third_out.at[rows, :], third_in.at[j - 1], g3_s.at[j], g3_r.at[j], zs[j])

    for j in (4, 3, 5, 2, 6, 1, 7):
        g3(j).start()
    final = piece[pl.ds(pl.multiple_of(z * 16, 16), 16), :]
    for j in (1, 7, 2, 6, 3, 5, 4):
        g3(j).wait_recv()
        final = final + third_in[j - 1].astype(F32)
    col = (1 - c) * (y * 1024 + xl * 512) + c * (xl * 2048 + y * 512)
    part = pg_ref.at[:, pl.ds(pl.multiple_of(col, 512), 512)]
    part[...] = final * SCALE
    g4 = {j: send(part, part, g4_s.at[j], g4_r.at[j], dps[j]) for j in dps}
    for j in g4:
        g4[j].start()

    @pl.when(c == 0)
    def _():
        for j in order[:3]:
            g1y(j)[1].wait_send()

    @pl.when(c == 1)
    def _():
        for j in order[:3]:
            g1x(j)[2].wait_send()

    for j in order[:3]:
        g2(j, peer).wait_send()
    for j in zs:
        g3(j).wait_send()
    for copy in outs:
        copy.wait()
    for j in g4:
        g4[j].wait()


def body(queries, teacher_queries, passages, bank_student, bank_teacher, owner, positives, keep):
    hbm = pl.BlockSpec(memory_space=pl.ANY)
    vmem = pl.BlockSpec(memory_space=pltpu.VMEM)
    dma = pltpu.SemaphoreType.DMA
    loss, query_grad, passage_grad = pl.pallas_call(
        kernel,
        out_shape=(
            jax.ShapeDtypeStruct((4, 128), F32),
            jax.ShapeDtypeStruct((512, E), BF),
            jax.ShapeDtypeStruct((16, E), F32),
        ),
        in_specs=[pl.BlockSpec(memory_space=pltpu.SMEM), hbm, hbm, hbm, hbm, hbm, vmem, hbm],
        out_specs=(vmem, hbm, vmem),
        scratch_shapes=[
            pltpu.VMEM((512, E), BF),
            pltpu.VMEM((512, E), BF),
            pltpu.VMEM((512, 256), jnp.int32),
            pltpu.VMEM((2, 256, E), BF),
            pltpu.VMEM((PIECES, 256, CW), BF),
            pltpu.VMEM((PIECES, 256, CW), BF),
            pltpu.VMEM((S - L, 16, CW), BF),
            pltpu.VMEM((N + L, 16, CW), BF),
            pltpu.VMEM((2, S, 16, CW), BF),
            pltpu.VMEM((512, 512), F32),
            pltpu.VMEM((256, 512), F32),
            pltpu.VMEM((256, 512), F32),
            pltpu.VMEM((512, 512), BF),
            pltpu.VMEM((512, 512), BF),
            pltpu.VMEM((512, 256), BF),
            pltpu.VMEM((256, E), BF),
            pltpu.VMEM((256, E), BF),
            pltpu.VMEM((256, E), F32),
            pltpu.VMEM((256, E), BF),
            pltpu.VMEM((3, 256, 1024), BF),
            pltpu.VMEM((3, 128, 2048), BF),
            pltpu.VMEM((3, 128, 512), BF),
            pltpu.VMEM((3, 128, 512), BF),
            pltpu.VMEM((128, 512), F32),
            pltpu.VMEM((128, 512), BF),
            pltpu.VMEM((7, 16, 512), BF),
            dma((4,)), dma((PIECES,)), dma((PIECES,)), dma((PIECES,)),
            dma((S - L,)), dma((S - L,)), dma((N + L,)), dma((N + L,)), dma((NB,)), dma((NB,)),
            dma((8,)), dma((8,)), dma((4,)), dma((4,)), dma((4,)), dma((4,)), dma, dma,
            dma((4,)), dma((4,)), dma((4,)), dma((4,)), dma((4,)), dma((4,)),
            dma((8,)), dma((8,)), dma((8,)), dma((8,)), dma((PARTS,)),
        ],
        compiler_params=pltpu.CompilerParams(
            collective_id=0, has_side_effects=True, vmem_limit_bytes=60 << 20
        ),
        name="distill_step",
    )(
        owner, queries, teacher_queries, passages, bank_student, bank_teacher,
        positives.reshape(1, 512), keep,
    )
    return loss.reshape(512), query_grad, passage_grad


def solution(mesh):
    torus = Mesh(mesh.devices.reshape(8, 2, 2, 4, 2), AXES)
    in_specs = (
        P(AXES, None),
        P(AXES, None),
        P(WIDE, None),
        P(WIDE, None),
        P(WIDE, None),
        P(DP),
        P(AXES),
        P(AXES, None),
    )
    out_specs = (P(AXES), P(AXES, None), P(WIDE, None))
    return jax.shard_map(body, mesh=torus, in_specs=in_specs, out_specs=out_specs, check_vma=False)
```
